32 devices in a mesh: pts: 8 (over y, x, core), out: 4 (over z).
Axes of the slice: x: 2, y: 2, z: 4, core: 2. Of those that a mesh axis runs over, the one named last changes fastest.
Arguments:
- points: bfloat16 [32768, 1024], P('pts'), may hold values from -6 to 6
- coefficients: float32 [32768, 1024], P('pts', 'out'), may hold values from -4 to 4
- residual: float32 [32768, 1024], P('pts', 'out'), may hold values from -6 to 6
- blocks: int32 [3, 512], replicated, may hold values from 0 to 32767, as said below
Outputs:
- coefficients_out: float32 [32768, 1024], P('pts', 'out')
- residual_out: float32 [32768, 1024], P('pts', 'out')
The draws below stay inside these ranges and needn't reach their ends.
Inputs may be any that keep to these rules, and one draw needn't show every extreme that they name: `blocks`: the 512 indices of a step are distinct.
All inputs are finite; a program needn't handle non-finite values.
Results may differ from the reference program's by a relative error of at most 0.0003.
Values may be sent and summed in bfloat16 or wider, within the bound.
No kernel may reach another device: no remote copies, remote signals or barrier semaphores. Data moves between devices by JAX's collectives and lax.ppermute only.
A program may use at most 128 MiB of HBM per device.

```python
import jax
import jax.numpy as jnp
from jax import lax

F = 1024
OUTS = 1024
B = 512
STEPS = 3
NPTS = 32768


def draw_blocks(key, part):
    picked = []
    for number in range(STEPS):
        shuffled = jax.random.permutation(jax.random.fold_in(key, 17 + number), NPTS)
        picked.append(shuffled[:B].astype(jnp.int32))
    return jnp.stack(picked)


def draw_points(key, part):
    base = jax.random.fold_in(key, 41)
    sign_key, mix_key, core_key, wide_key, noise_key = jax.random.split(base, 5)
    signs = jnp.where(jax.random.uniform(sign_key, (3, F), jnp.float32) < 0.5, -1.0, 1.0).astype(jnp.float32)
    core_share = 0.7
    reach = 1.5
    noise = 0.1 * jax.random.normal(noise_key, (NPTS, F), jnp.float32)
    core = 0.03 * jax.random.normal(core_key, (NPTS, 3), jnp.float32)
    wide = jax.random.uniform(wide_key, (NPTS, 3), jnp.float32, -reach, reach)
    in_core = jax.random.uniform(mix_key, (NPTS, 1), jnp.float32) < core_share
    coords = jnp.where(in_core, core, wide)
    values = jnp.dot(coords, signs, precision=lax.Precision.HIGHEST) + noise
    return jnp.clip(values, -6.0, 6.0).astype(jnp.bfloat16)


def steps_of(stream_key, extent, pieces, least, largest):
    gain, own = 1.0, jax.random.fold_in(stream_key, 6)
    for position, parts in pieces:
        steps = jnp.exp(jax.random.uniform(jax.random.fold_in(own, position), (parts,), jnp.float32, least / len(pieces), largest / len(pieces)))
        gain = gain * jnp.repeat(steps, extent[position] // parts).reshape([-1 if axis == position else 1 for axis in range(len(extent))])
    return gain


def bell_draw(key, dims, width, limit, cuts=(), kind=jnp.bfloat16):
    array = jax.random.normal(key, dims, jnp.float32) * width
    if len(cuts) > 0:
        array = steps_of(key, dims, cuts, -0.22, 0.18) * array
    return jnp.clip(array, min=-limit, max=limit).astype(kind)


def setup_inputs(seed: int = 0) -> dict:
    splits = jax.random.split(jax.random.key(seed), 5)
    return {
        "points": draw_points(jax.random.fold_in(splits[4], 71), 0),
        "coefficients": bell_draw(splits[1], (NPTS, OUTS), 0.5, 4.0, ((0, 8), (1, 4)), jnp.float32),
        "residual": bell_draw(splits[2], (NPTS, OUTS), 1.0, 6.0, ((0, 8), (1, 4)), jnp.float32),
        "blocks": draw_blocks(jax.random.fold_in(splits[4], 71), 0),
    }


RIDGE = 0.5

def kernel(left_rows, right_rows, inverse_width):
    left_sq = jnp.sum(jnp.square(left_rows.astype(jnp.float32)), axis=1)
    right_sq = jnp.sum(jnp.square(right_rows.astype(jnp.float32)), axis=1)
    inner = lax.dot_general(left_rows.astype(jnp.float32), right_rows.astype(jnp.float32), (((1,), (1,)), ((), ())), preferred_element_type=jnp.float32)
    return jnp.exp(-inverse_width * (left_sq[:, None] + right_sq[None, :] - 2.0 * inner))

def reference(points, coefficients, residual, blocks):
    inverse_width = 1.0 / F
    for number in range(STEPS):
        chosen = blocks[number]
        block_pts = points[chosen]
        kernel_rows = kernel(points, block_pts, inverse_width)
        block_kernel = kernel_rows[chosen] + RIDGE * jnp.eye(B, dtype=jnp.float32)
        block_res = residual[chosen]
        factor = jnp.linalg.cholesky(block_kernel)
        update = jax.scipy.linalg.cho_solve((factor, True), block_res)
        coefficients = coefficients.at[chosen].add(update)
        placed = jnp.zeros_like(residual).at[chosen].add(update)
        residual = residual - jnp.dot(kernel_rows, update, precision=lax.Precision.HIGHEST) - RIDGE * placed
    return (coefficients, residual)
```

```python
import functools

import jax
import jax.numpy as jnp
from jax import lax
from jax.experimental import pallas as pl
from jax.experimental.pallas import tpu as pltpu
from jax.sharding import PartitionSpec as P

RIDGE = 0.5
PANEL = 128
GROUP = 4
HIGHEST = lax.Precision.HIGHEST
NT = (((1,), (1,)), ((), ()))
TN = (((0,), (0,)), ((), ()))


def dot32(a, b, dims=(((1,), (0,)), ((), ()))):
    return lax.dot_general(a, b, dims, precision=HIGHEST, preferred_element_type=jnp.float32)


def spread_lane(tile, lane):
    return jnp.broadcast_to(tile[:, lane : lane + 1], tile.shape)


def spread_row(tile, row):
    return jnp.broadcast_to(tile[row : row + 1, :], tile.shape)


def eliminate(tiles, start):
    lanes = lax.broadcasted_iota(jnp.int32, (8, PANEL), 1)
    subs = lax.broadcasted_iota(jnp.int32, (8, PANEL), 0)
    first, offset = start // 8, start % 8
    in_group = (lanes >= start) & (lanes < start + GROUP)
    head = tiles[first]
    columns = [[spread_lane(tiles[t], start + q) for t in range(first, len(tiles))] for q in range(GROUP)]
    rows = []
    for q in range(GROUP):
        own = jnp.where(lanes == start + q, 1.0, 0.0)
        rows.append(jnp.where(in_group, own, spread_row(head, offset + q)))
    pivot = {}
    for m in range(GROUP):
        for q in range(m, GROUP):
            pivot[q, m] = spread_row(columns[m][0], offset + q)
    roots, scaled = [], []
    for m in range(GROUP):
        root = lax.rsqrt(pivot[m, m])
        inverse = root * root
        roots.append(root)
        factor = {q: pivot[q, m] * inverse for q in range(m + 1, GROUP)}
        for q in range(m + 1, GROUP):
            for n in range(m + 1, q + 1):
                pivot[q, n] = pivot[q, n] - factor[q] * pivot[n, m]
        for q in range(m + 1, GROUP):
            rows[q] = rows[q] - factor[q] * rows[m]
            columns[q] = [c - factor[q] * b for c, b in zip(columns[q], columns[m])]
        scaled.append(rows[m] * inverse)
    out = list(tiles)
    for t in range(first, len(tiles)):
        if t == first and offset + GROUP == 8:
            continue
        value = jnp.where(in_group, 0.0, tiles[t])
        for m in range(GROUP):
            value = value - columns[m][t - first] * scaled[m]
        out[t] = value
    top = jnp.where(subs < offset, head, out[first])
    for m in range(GROUP):
        done = jnp.where(lanes < start + GROUP, rows[m] * roots[m], 0.0)
        top = jnp.where(subs == offset + m, done, top)
    out[first] = top
    return out


def factor_kernel(steps, size, scale, points_ref, col_ref, row_ref, inv_ref, cross_ref, norm_ref, work):
    def rows_of(s):
        return points_ref[s * size : (s + 1) * size, :]

    eye = lax.broadcasted_iota(jnp.int32, (size, size), 0) == lax.broadcasted_iota(jnp.int32, (size, size), 1)
    norm_cols = []
    for s in range(steps):
        inner = lax.dot_general(rows_of(s), rows_of(s), NT, preferred_element_type=jnp.float32)
        diagonal = jnp.where(eye, inner, 0.0)
        norm_col = jnp.sum(diagonal, axis=1, keepdims=True)
        norm_row = jnp.sum(diagonal, axis=0, keepdims=True)
        norm_cols.append(norm_col)
        norm_ref[:, s * size : (s + 1) * size] = norm_row
        work[s] = jnp.exp((2.0 * inner - norm_col - norm_row) * scale) + jnp.where(eye, RIDGE, 0.0)
    pair = 0
    for s in range(steps):
        for t in range(s):
            inner = lax.dot_general(rows_of(s), rows_of(t), NT, preferred_element_type=jnp.float32)
            norm_row = norm_ref[:, t * size : (t + 1) * size]
            same = col_ref[s * size : (s + 1) * size, :] == row_ref[:, t * size : (t + 1) * size]
            cross_ref[pair] = jnp.exp((2.0 * inner - norm_cols[s] - norm_row) * scale) + jnp.where(same, RIDGE, 0.0)
            pair += 1
    panels = size // PANEL
    for k in range(panels):
        low, high = k * PANEL, (k + 1) * PANEL
        blocks = []
        for s in range(steps):
            blocks.append([work[s, low + 8 * t : low + 8 * t + 8, low:high] for t in range(PANEL // 8)])
        for start in range(0, PANEL, GROUP):
            blocks = [eliminate(tiles, start) for tiles in blocks]
        for s in range(steps):
            inv_ref[s, low:high, low:high] = jnp.concatenate(blocks[s], axis=0)
        for s in range(steps):
            tri = inv_ref[s, low:high, low:high]
            if high < size:
                inv_ref[s, low:high, high:] = jnp.zeros((PANEL, size - high), jnp.float32)
                below = dot32(work[s, high:, low:high], tri, NT)
                work[s, high:, low:high] = below
                work[s, high:, high:] = work[s, high:, high:] - dot32(below, below, NT)
            if low > 0:
                left = dot32(work[s, low:high, :low], inv_ref[s, :low, :low])
                inv_ref[s, low:high, :low] = -dot32(tri, left)


def solve_kernel(steps, size, inv_ref, cross_ref, res_ref, up_ref, high_ref, low_ref, half_ref):
    pair = 0
    total = None
    for s in range(steps):
        here = slice(s * size, (s + 1) * size)
        rhs = res_ref[here, :]
        for t in range(s):
            rhs = rhs - dot32(cross_ref[pair], up_ref[t * size : (t + 1) * size, :])
            pair += 1
        update = dot32(inv_ref[s], dot32(inv_ref[s], rhs), TN)
        up_ref[here, :] = update
        high = update.astype(jnp.bfloat16)
        high_ref[here, :] = high
        low_ref[here, :] = (update - high.astype(jnp.float32)).astype(jnp.bfloat16)
        part = jnp.sum(update, axis=0, keepdims=True)
        total = part if total is None else total + part
    half_ref[...] = 0.5 * total


def apply_kernel(scale, tile, points_ref, chosen_ref, norm_ref, row_ref, high_ref, low_ref, half_ref, res_ref, out_ref):
    mine = points_ref[...]
    wide = mine.astype(jnp.float32)
    norm_col = jnp.sum(wide * wide, axis=1, keepdims=True)
    inner = lax.dot_general(mine, chosen_ref[...], NT, preferred_element_type=jnp.float32)
    ids = lax.broadcasted_iota(jnp.int32, (tile, 1), 0) + pl.program_id(0) * tile
    shifted = jnp.where(ids == row_ref[...], RIDGE - 0.5, -0.5)
    values = jnp.exp((2.0 * inner - norm_col - norm_ref[...]) * scale) + shifted
    high = values.astype(jnp.bfloat16)
    low = (values - high.astype(jnp.float32)).astype(jnp.bfloat16)
    product = jnp.dot(high, high_ref[...], preferred_element_type=jnp.float32)
    product += jnp.dot(high, low_ref[...], preferred_element_type=jnp.float32)
    product += jnp.dot(low, high_ref[...], preferred_element_type=jnp.float32)
    out_ref[...] = res_ref[...] - product - half_ref[...]


def local(points, coefficients, residual, blocks):
    local_count, features = points.shape
    outs = residual.shape[1]
    steps, size = blocks.shape
    scale = 1.0 / features
    position = lax.axis_index("pts")
    offsets = blocks.reshape(-1) - position * local_count
    is_owned = (offsets >= 0) & (offsets < local_count)
    clipped = jnp.clip(offsets, 0, local_count - 1)
    owned_rows = jnp.where(is_owned[:, None], points[clipped], jnp.bfloat16(0.0))
    owned_res = jnp.where(is_owned[:, None], residual[clipped], 0.0)
    chosen = lax.psum(owned_rows, "pts")
    block_res = lax.psum(owned_res, "pts")

    count = steps * size
    pairs = steps * (steps - 1) // 2
    f32 = jnp.float32
    params = pltpu.CompilerParams(vmem_limit_bytes=60 * 2**20)
    inverse, cross, norms = pl.pallas_call(
        functools.partial(factor_kernel, steps, size, scale),
        out_shape=(
            jax.ShapeDtypeStruct((steps, size, size), f32),
            jax.ShapeDtypeStruct((pairs, size, size), f32),
            jax.ShapeDtypeStruct((1, count), f32),
        ),
        scratch_shapes=[pltpu.VMEM((steps, size, size), f32)],
        compiler_params=params,
        name="factor",
    )(chosen, offsets[:, None], offsets[None, :])
    update, high, low, half = pl.pallas_call(
        functools.partial(solve_kernel, steps, size),
        out_shape=(
            jax.ShapeDtypeStruct((count, outs), f32),
            jax.ShapeDtypeStruct((count, outs), jnp.bfloat16),
            jax.ShapeDtypeStruct((count, outs), jnp.bfloat16),
            jax.ShapeDtypeStruct((1, outs), f32),
        ),
        compiler_params=params,
        name="solve",
    )(inverse, cross, block_res)
    tile = 512

    def whole(shape):
        return pl.BlockSpec(shape, lambda i: (0, 0), pipeline_mode=pl.Buffered(1))

    residual_out = pl.pallas_call(
        functools.partial(apply_kernel, scale, tile),
        grid=(local_count // tile,),
        in_specs=[
            pl.BlockSpec((tile, features), lambda i: (i, 0)),
            whole((count, features)),
            whole((1, count)),
            whole((1, count)),
            whole((count, outs)),
            whole((count, outs)),
            whole((1, outs)),
            pl.BlockSpec((tile, outs), lambda i: (i, 0)),
        ],
        out_specs=pl.BlockSpec((tile, outs), lambda i: (i, 0)),
        out_shape=jax.ShapeDtypeStruct((local_count, outs), f32),
        compiler_params=params,
        name="apply",
    )(points, chosen, norms, offsets[None, :], high, low, half, residual)
    own_update = jnp.where(is_owned[:, None], update, 0.0)
    coefficients = coefficients.at[clipped].add(own_update)
    return (coefficients, residual_out)


def solution(mesh):
    return jax.shard_map(
        local,
        mesh=mesh,
        in_specs=(P("pts", None), P("pts", "out"), P("pts", "out"), P()),
        out_specs=(P("pts", "out"), P("pts", "out")),
        check_vma=False,
    )
```

```python
import functools

import jax
import jax.numpy as jnp
from jax import lax
from jax.experimental import pallas as pl
from jax.experimental.pallas import tpu as pltpu
from jax.sharding import PartitionSpec as P

RIDGE = 0.5
PANEL = 128
GROUP = 4
HIGHEST = lax.Precision.HIGHEST
NT = (((1,), (1,)), ((), ()))
TN = (((0,), (0,)), ((), ()))


def dot32(a, b, dims=(((1,), (0,)), ((), ()))):
    return lax.dot_general(a, b, dims, precision=HIGHEST, preferred_element_type=jnp.float32)


def spread_lane(tile, lane):
    return jnp.broadcast_to(tile[:, lane : lane + 1], tile.shape)


def spread_row(tile, row):
    return jnp.broadcast_to(tile[row : row + 1, :], tile.shape)


def eliminate(tiles, start):
    lanes = lax.broadcasted_iota(jnp.int32, (8, PANEL), 1)
    subs = lax.broadcasted_iota(jnp.int32, (8, PANEL), 0)
    first, offset = start // 8, start % 8
    in_group = (lanes >= start) & (lanes < start + GROUP)
    head = tiles[first]
    columns = [[spread_lane(tiles[t], start + q) for t in range(first, len(tiles))] for q in range(GROUP)]
    rows = []
    for q in range(GROUP):
        own = jnp.where(lanes == start + q, 1.0, 0.0)
        rows.append(jnp.where(in_group, own, spread_row(head, offset + q)))
    pivot = {}
    for m in range(GROUP):
        for q in range(m, GROUP):
            pivot[q, m] = spread_row(columns[m][0], offset + q)
    roots, scaled = [], []
    for m in range(GROUP):
        root = lax.rsqrt(pivot[m, m])
        inverse = root * root
        roots.append(root)
        factor = {q: pivot[q, m] * inverse for q in range(m + 1, GROUP)}
        for q in range(m + 1, GROUP):
            for n in range(m + 1, q + 1):
                pivot[q, n] = pivot[q, n] - factor[q] * pivot[n, m]
        for q in range(m + 1, GROUP):
            rows[q] = rows[q] - factor[q] * rows[m]
            columns[q] = [c - factor[q] * b for c, b in zip(columns[q], columns[m])]
        scaled.append(rows[m] * inverse)
    out = list(tiles)
    for t in range(first, len(tiles)):
        if t == first and offset + GROUP == 8:
            continue
        value = jnp.where(in_group, 0.0, tiles[t])
        for m in range(GROUP):
            value = value - columns[m][t - first] * scaled[m]
        out[t] = value
    top = jnp.where(subs < offset, head, out[first])
    for m in range(GROUP):
        done = jnp.where(lanes < start + GROUP, rows[m] * roots[m], 0.0)
        top = jnp.where(subs == offset + m, done, top)
    out[first] = top
    return out


def factor_kernel(steps, size, *refs):
    grams, (inv_ref, work) = refs[:steps], refs[steps:]
    for s in range(steps):
        work[s] = grams[s][...]
    panels = size // PANEL
    for k in range(panels):
        low, high = k * PANEL, (k + 1) * PANEL
        blocks = []
        for s in range(steps):
            blocks.append([work[s, low + 8 * t : low + 8 * t + 8, low:high] for t in range(PANEL // 8)])
        for start in range(0, PANEL, GROUP):
            blocks = [eliminate(tiles, start) for tiles in blocks]
        for s in range(steps):
            inv_ref[s, low:high, low:high] = jnp.concatenate(blocks[s], axis=0)
        for s in range(steps):
            tri = inv_ref[s, low:high, low:high]
            if high < size:
                inv_ref[s, low:high, high:] = jnp.zeros((PANEL, size - high), jnp.float32)
                below = dot32(work[s, high:, low:high], tri, NT)
                work[s, high:, low:high] = below
                work[s, high:, high:] = work[s, high:, high:] - dot32(below, below, NT)
            if low > 0:
                left = dot32(work[s, low:high, :low], inv_ref[s, :low, :low])
                inv_ref[s, low:high, :low] = -dot32(tri, left)


def halves_of(ref, wide):
    parts, rest = [], ref
    for _ in range(wide):
        part = rest.astype(jnp.bfloat16)
        parts.append(part)
        rest = rest - part.astype(jnp.float32)
    return parts


def select_kernel(parts, tile, pick_ref, data_ref, left_ref, right_ref, total):
    step = pl.program_id(0)
    slots, half = total.shape[0], total.shape[1] // 2
    ids = lax.broadcasted_iota(jnp.int32, (slots, tile), 1) + step * tile
    chosen = jnp.where(ids == pick_ref[...], 1.0, 0.0).astype(jnp.bfloat16)
    data = data_ref[...]
    pieces = [data] if parts == 1 else halves_of(data, parts)
    value = jnp.dot(chosen, pieces[0], preferred_element_type=jnp.float32)
    for piece in pieces[1:]:
        value += jnp.dot(chosen, piece, preferred_element_type=jnp.float32)

    @pl.when(step == 0)
    def _():
        total[...] = value

    @pl.when(step > 0)
    def _():
        total[...] += value

    @pl.when(step == pl.num_programs(0) - 1)
    def _():
        left_ref[...] = total[:, :half].astype(left_ref.dtype)
        right_ref[...] = total[:, half:].astype(right_ref.dtype)


def place_kernel(parts, steps, size, devices, *refs):
    if len(refs) == 6:
        base_ref, refs = refs[0], refs[1:]
    else:
        base_ref = None
    slots, places, out_ref = refs[:2], refs[2:4], refs[4]
    room = slots[0].shape[1] // steps
    half = slots[0].shape[2]
    lanes = lax.broadcasted_iota(jnp.int32, (size, devices * room), 1)
    for s in range(steps):
        here = slice(s * size, (s + 1) * size)
        for side in range(2):
            source = slots[side][:, s * room : (s + 1) * room, :].reshape(devices * room, half)
            chosen = jnp.where(lanes == places[side][here, :], 1.0, 0.0).astype(jnp.bfloat16)
            pieces = [source] if parts == 1 else halves_of(source, parts)
            value = jnp.dot(chosen, pieces[0], preferred_element_type=jnp.float32)
            for piece in pieces[1:]:
                value += jnp.dot(chosen, piece, preferred_element_type=jnp.float32)
            columns = slice(side * half, (side + 1) * half)
            if base_ref is not None:
                value += base_ref[here, columns].astype(jnp.float32)
            out_ref[here, columns] = value.astype(out_ref.dtype)


def gauss(inner, left, right, scale):
    return jnp.exp2((inner - left - right) * (2.0 * scale * 1.4426950408889634))


def rows_kernel(steps, size, scale, tile, points_ref, col_ref, row_ref, chosen_ref, *refs):
    pairs = steps * (steps - 1) // 2
    high_ref, low_ref = refs[:2]
    grams, crosses = refs[2 : 2 + steps], refs[2 + steps : 2 + steps + pairs]
    inner_ref, half_ref, norm_ref = refs[2 + steps + pairs :]
    step = pl.program_id(0)

    def block(s):
        return slice(s * size, (s + 1) * size)

    @pl.when(step == 0)
    def _():
        eye = lax.broadcasted_iota(jnp.int32, (size, size), 0) == lax.broadcasted_iota(jnp.int32, (size, size), 1)
        columns = []
        for s in range(steps):
            inner = lax.dot_general(chosen_ref[block(s), :], chosen_ref[block(s), :], NT, preferred_element_type=jnp.float32)
            diagonal = jnp.where(eye, inner, 0.0)
            column = 0.5 * jnp.sum(diagonal, axis=1, keepdims=True)
            line = 0.5 * jnp.sum(diagonal, axis=0, keepdims=True)
            columns.append(column)
            norm_ref[:, block(s)] = line
            grams[s][...] = gauss(inner, column, line, scale) + jnp.where(eye, RIDGE, 0.0)
        pair = 0
        for s in range(steps):
            for t in range(s):
                inner = lax.dot_general(chosen_ref[block(s), :], chosen_ref[block(t), :], NT, preferred_element_type=jnp.float32)
                same = col_ref[block(s), :] == row_ref[:, block(t)]
                crosses[pair][...] = gauss(inner, columns[s], norm_ref[:, block(t)], scale) + jnp.where(same, RIDGE, 0.0)
                pair += 1

    now, before = step % 2, (step + 1) % 2
    rows = points_ref[...]
    wide = rows.astype(jnp.float32)
    half_ref[now] = 0.5 * jnp.sum(wide * wide, axis=1, keepdims=True)
    inner_ref[now] = lax.dot_general(rows, chosen_ref[...], NT, preferred_element_type=jnp.float32)
    values = gauss(inner_ref[before], half_ref[before], norm_ref[...], scale) - 0.5
    high = values.astype(jnp.bfloat16)
    high_ref[...] = high
    low_ref[...] = (values - high.astype(jnp.float32)).astype(jnp.bfloat16)


def solve_kernel(steps, size, *refs):
    pairs = steps * (steps - 1) // 2
    inv_ref, crosses, res_ref = refs[0], refs[1 : 1 + pairs], refs[1 + pairs]
    up_ref, high_ref, low_ref, half_ref, work = refs[2 + pairs :]
    pair = 0
    total = None
    mid = size // 2
    for s in range(steps):
        here = slice(s * size, (s + 1) * size)
        rhs = res_ref[here, :]
        for t in range(s):
            rhs = rhs - dot32(crosses[pair][...], up_ref[t * size : (t + 1) * size, :])
            pair += 1
        work[:mid, :] = dot32(inv_ref[s, :mid, :mid], rhs[:mid])
        work[mid:, :] = dot32(inv_ref[s, mid:, :], rhs)
        upper = dot32(inv_ref[s, :, :mid], work[...], TN)
        lower = dot32(inv_ref[s, mid:, mid:], work[mid:, :], TN)
        for begin, update in ((s * size, upper), (s * size + mid, lower)):
            part = slice(begin, begin + mid)
            up_ref[part, :] = update
            high = update.astype(jnp.bfloat16)
            high_ref[part, :] = high
            low_ref[part, :] = (update - high.astype(jnp.float32)).astype(jnp.bfloat16)
            partial = jnp.sum(update, axis=0, keepdims=True)
            total = partial if total is None else total + partial
    half_ref[...] = 0.5 * total


def apply_kernel(tile, order_ref, place_ref, bound_ref, *refs):
    k_high, k_low, high_ref, low_ref, up_ref, half_ref, res_ref, coef_ref, res_out, coef_out = refs
    value = jnp.dot(k_high[...], high_ref[...], preferred_element_type=jnp.float32)
    value += jnp.dot(k_high[...], low_ref[...], preferred_element_type=jnp.float32)
    value += jnp.dot(k_low[...], high_ref[...], preferred_element_type=jnp.float32)
    res_out[...] = res_ref[...] - half_ref[...] - value
    coef_out[...] = coef_ref[...]
    step = pl.program_id(0)

    def add_row(slot, carry):
        row = place_ref[slot] - step * tile
        update = up_ref[pl.ds(order_ref[slot], 1), :]
        coef_out[pl.ds(row, 1), :] += update
        res_out[pl.ds(row, 1), :] -= RIDGE * update
        return carry

    lax.fori_loop(bound_ref[step], bound_ref[step + 1], add_row, 0)


def swap(block, bit, count):
    return lax.ppermute(block, "pts", [(i, i ^ bit) for i in range(count)])


def gather_slots(block, order, count):
    value = block[None]
    for bit in order:
        value = jnp.concatenate([value, swap(value, bit, count)], axis=0)
    return value


def route(order):
    names = [0]
    for bit in order:
        names = names + [name ^ bit for name in names]
    return names


def local(points, coefficients, residual, blocks):
    local_count, features = points.shape
    outs = residual.shape[1]
    steps, size = blocks.shape
    scale = 1.0 / features
    devices = lax.axis_size("pts")
    position = lax.axis_index("pts")
    count = steps * size
    pairs = steps * (steps - 1) // 2
    f32, bf16, i32 = jnp.float32, jnp.bfloat16, jnp.int32
    params = pltpu.CompilerParams(vmem_limit_bytes=60 * 2**20)
    tile = 512
    tiles = local_count // tile

    def shape(dims, kind=f32):
        return jax.ShapeDtypeStruct(dims, kind)

    def whole(dims):
        return pl.BlockSpec(dims, lambda i, *_: (0,) * len(dims), pipeline_mode=pl.Buffered(1))

    def striped(width):
        return pl.BlockSpec((tile, width), lambda i, *_: (i, 0))

    mean = size // devices
    room = -(-(mean + 4 * int(mean**0.5 + 0.999)) // 16) * 16
    owner = blocks // local_count
    earlier = jnp.arange(size)[:, None] > jnp.arange(size)[None, :]
    rank = jnp.sum((owner[:, :, None] == owner[:, None, :]) & earlier, axis=2, dtype=i32)
    rounds = jnp.max(rank) // room + 1
    offsets = blocks - position * local_count
    is_owned = owner == position
    bits = [1 << b for b in range(devices.bit_length() - 1)]
    orders = (bits[1:] + bits[:1], bits[:0:-1] + bits[:1])
    slot_ids = jnp.arange(room, dtype=i32)

    def exchange(number, data, base):
        parts = 1 if data.dtype == bf16 else 3
        width = data.shape[1]
        within = rank - number * room
        taken = is_owned[:, None, :] & (within[:, None, :] == slot_ids[None, :, None])
        pick = jnp.max(jnp.where(taken, offsets[:, None, :], -1), axis=2).reshape(steps * room, 1)
        sides = pl.pallas_call(
            functools.partial(select_kernel, parts, tile),
            grid=(tiles,),
            in_specs=[whole((steps * room, 1)), striped(width)],
            out_specs=[whole((steps * room, width // 2))] * 2,
            out_shape=[shape((steps * room, width // 2), data.dtype)] * 2,
            scratch_shapes=[pltpu.VMEM((steps * room, width), f32)],
            compiler_params=params,
            cost_estimate=pl.CostEstimate(
                flops=2 * parts * steps * room * local_count * width,
                bytes_accessed=data.size * data.dtype.itemsize,
                transcendentals=0,
            ),
            name=f"select{parts}",
        )(pick, data)
        fits = (within >= 0) & (within < room)
        gathered, places = [], []
        for side, order in zip(sides, orders):
            gathered.append(gather_slots(side, order, devices))
            inverse = [0] * devices
            for index, name in enumerate(route(order)):
                inverse[name] = index
            relative = owner ^ position
            index = jnp.sum(jnp.where(relative[..., None] == jnp.arange(devices), jnp.array(inverse, i32), 0), axis=-1)
            places.append(jnp.where(fits, index * room + within, -1).reshape(count, 1))
        extra = [] if base is None else [base]
        return pl.pallas_call(
            functools.partial(place_kernel, parts, steps, size, devices),
            out_shape=shape((count, width), data.dtype),
            compiler_params=params,
            cost_estimate=pl.CostEstimate(
                flops=2 * parts * count * devices * room * width,
                bytes_accessed=2 * count * width * data.dtype.itemsize,
                transcendentals=0,
            ),
            name=f"place{parts}",
        )(*extra, *gathered, *places)

    def more(number, state):
        return (exchange(number, points, state[0]), exchange(number, residual, state[1]))

    chosen = exchange(0, points, None)
    block_res = exchange(0, residual, None)
    chosen, block_res = lax.fori_loop(1, rounds, more, (chosen, block_res))

    flat = offsets.reshape(-1)
    mine = is_owned.reshape(-1)
    key = jnp.where(mine, flat * count + jnp.arange(count), -1)
    turn = jnp.sum((key[None, :] >= 0) & (key[None, :] < key[:, None]), axis=1)
    slots = jnp.arange(count)[:, None]
    here = mine[None, :] & (turn[None, :] == slots)
    order = jnp.sum(jnp.where(here, jnp.arange(count)[None, :], 0), axis=1)
    place = jnp.sum(jnp.where(here, flat[None, :], 0), axis=1)
    edges = jnp.arange(tiles + 1) * tile
    bound = jnp.sum(mine[None, :] & (flat[None, :] < edges[:, None]), axis=1)

    def behind(width):
        return pl.BlockSpec((tile, width), lambda i: (jnp.maximum(i - 1, 0), 0))

    result = pl.pallas_call(
        functools.partial(rows_kernel, steps, size, scale, tile),
        grid=(tiles + 1,),
        in_specs=[
            pl.BlockSpec((tile, features), lambda i: (jnp.minimum(i, tiles - 1), 0)),
            whole((count, 1)),
            whole((1, count)),
            whole((count, features)),
        ],
        out_specs=[behind(count)] * 2 + [whole((size, size))] * (steps + pairs),
        out_shape=[shape((local_count, count), bf16)] * 2 + [shape((size, size))] * (steps + pairs),
        scratch_shapes=[
            pltpu.VMEM((2, tile, count), f32),
            pltpu.VMEM((2, tile, 1), f32),
            pltpu.VMEM((1, count), f32),
        ],
        compiler_params=params,
        cost_estimate=pl.CostEstimate(
            flops=2 * (local_count + count) * count * features,
            bytes_accessed=2 * local_count * (features + 2 * count),
            transcendentals=local_count * count,
        ),
        name="rows",
    )(points, flat[:, None], flat[None, :], chosen)
    k_high, k_low = result[:2]
    grams, crosses = result[2 : 2 + steps], result[2 + steps :]
    inverse = pl.pallas_call(
        functools.partial(factor_kernel, steps, size),
        out_shape=shape((steps, size, size)),
        scratch_shapes=[pltpu.VMEM((steps, size, size), f32)],
        compiler_params=params,
        cost_estimate=pl.CostEstimate(flops=2 * 10**10, bytes_accessed=4 * count * size * 2, transcendentals=0),
        name="factor",
    )(*grams)
    update, high, low, half = pl.pallas_call(
        functools.partial(solve_kernel, steps, size),
        out_shape=(shape((count, outs)), shape((count, outs), bf16), shape((count, outs), bf16), shape((1, outs))),
        scratch_shapes=[pltpu.VMEM((size, outs), f32)],
        compiler_params=params,
        name="solve",
    )(inverse, *crosses, block_res)
    residual_out, coefficients_out = pl.pallas_call(
        functools.partial(apply_kernel, tile),
        grid_spec=pltpu.PrefetchScalarGridSpec(
            num_scalar_prefetch=3,
            grid=(tiles,),
            in_specs=[striped(count)] * 2
            + [whole((count, outs))] * 3
            + [whole((1, outs))]
            + [striped(outs)] * 2,
            out_specs=[striped(outs)] * 2,
        ),
        out_shape=[shape((local_count, outs))] * 2,
        compiler_params=params,
        name="apply",
    )(order, place, bound, k_high, k_low, high, low, update, half, residual, coefficients)
    return (coefficients_out, residual_out)


def solution(mesh):
    return jax.shard_map(
        local,
        mesh=mesh,
        in_specs=(P("pts", None), P("pts", "out"), P("pts", "out"), P()),
        out_specs=(P("pts", "out"), P("pts", "out")),
        check_vma=False,
    )
```

```python
import functools

import jax
import jax.numpy as jnp
from jax import lax
from jax.experimental import pallas as pl
from jax.experimental.pallas import tpu as pltpu
from jax.sharding import PartitionSpec as P

RIDGE = 0.5
PANEL = 128
GROUP = 4
CHUNK = 256
PIECE = 256
HIGHEST = lax.Precision.HIGHEST
NT = (((1,), (1,)), ((), ()))
TN = (((0,), (0,)), ((), ()))


def dot32(a, b, dims=(((1,), (0,)), ((), ()))):
    return lax.dot_general(a, b, dims, precision=HIGHEST, preferred_element_type=jnp.float32)


def spread_lane(tile, lane):
    return jnp.broadcast_to(tile[:, lane : lane + 1], tile.shape)


def spread_row(tile, row):
    return jnp.broadcast_to(tile[row : row + 1, :], tile.shape)


def eliminate(tiles, start):
    lanes = lax.broadcasted_iota(jnp.int32, (8, PANEL), 1)
    subs = lax.broadcasted_iota(jnp.int32, (8, PANEL), 0)
    first, offset = start // 8, start % 8
    in_group = (lanes >= start) & (lanes < start + GROUP)
    head = tiles[first]
    columns = [[spread_lane(tiles[t], start + q) for t in range(first, len(tiles))] for q in range(GROUP)]
    rows = []
    for q in range(GROUP):
        own = jnp.where(lanes == start + q, 1.0, 0.0)
        rows.append(jnp.where(in_group, own, spread_row(head, offset + q)))
    pivot = {}
    for m in range(GROUP):
        for q in range(m, GROUP):
            pivot[q, m] = spread_row(columns[m][0], offset + q)
    roots, scaled = [], []
    for m in range(GROUP):
        root = lax.rsqrt(pivot[m, m])
        inverse = root * root
        roots.append(root)
        factor = {q: pivot[q, m] * inverse for q in range(m + 1, GROUP)}
        for q in range(m + 1, GROUP):
            for n in range(m + 1, q + 1):
                pivot[q, n] = pivot[q, n] - factor[q] * pivot[n, m]
        for q in range(m + 1, GROUP):
            rows[q] = rows[q] - factor[q] * rows[m]
            columns[q] = [c - factor[q] * b for c, b in zip(columns[q], columns[m])]
        scaled.append(rows[m] * inverse)
    out = list(tiles)
    for t in range(first, len(tiles)):
        if t == first and offset + GROUP == 8:
            continue
        value = jnp.where(in_group, 0.0, tiles[t])
        for m in range(GROUP):
            value = value - columns[m][t - first] * scaled[m]
        out[t] = value
    top = jnp.where(subs < offset, head, out[first])
    for m in range(GROUP):
        done = jnp.where(lanes < start + GROUP, rows[m] * roots[m], 0.0)
        top = jnp.where(subs == offset + m, done, top)
    out[first] = top
    return out


def factor(steps, size, work, inv_ref):
    panels = size // PANEL
    for k in range(panels):
        low, high = k * PANEL, (k + 1) * PANEL
        blocks = []
        for s in range(steps):
            blocks.append([work[s, low + 8 * t : low + 8 * t + 8, low:high] for t in range(PANEL // 8)])
        for start in range(0, PANEL, GROUP):
            blocks = [eliminate(tiles, start) for tiles in blocks]
        for s in range(steps):
            inv_ref[s, low:high, low:high] = jnp.concatenate(blocks[s], axis=0)
        for s in range(steps):
            tri = inv_ref[s, low:high, low:high]
            if high < size:
                inv_ref[s, low:high, high:] = jnp.zeros((PANEL, size - high), jnp.float32)
                below = dot32(work[s, high:, low:high], tri, NT)
                work[s, high:, low:high] = below
                work[s, high:, high:] = work[s, high:, high:] - dot32(below, below, NT)
            if low > 0:
                left = dot32(work[s, low:high, :low], inv_ref[s, :low, :low])
                inv_ref[s, low:high, :low] = -dot32(tri, left)


def column_of(row):
    size = row.shape[1]
    eye = lax.broadcasted_iota(jnp.int32, (size, size), 0) == lax.broadcasted_iota(jnp.int32, (size, size), 1)
    return jnp.sum(jnp.where(eye, row, 0.0), axis=1, keepdims=True)


def rank_row(owner):
    size = owner.shape[1]
    earlier = lax.broadcasted_iota(jnp.int32, (size, size), 0) < lax.broadcasted_iota(jnp.int32, (size, size), 1)
    return jnp.sum(jnp.where((column_of(owner) == owner) & earlier, 1.0, 0.0), axis=0, keepdims=True)


def split2(value):
    high = value.astype(jnp.bfloat16)
    return high, (value - high.astype(jnp.float32)).astype(jnp.bfloat16)


def select_kernel(steps, size, room, number_ref, table_ref, points_ref, res_ref, left_ref, right_ref, pick, total):
    step = pl.program_id(0)
    reach, features = points_ref.shape
    outs = res_ref.shape[1]
    slots, half = steps * room, features // 2

    @pl.when(step == 0)
    def _():
        first = (number_ref[0] * room).astype(jnp.float32)
        for s in range(steps):
            here = slice(s * size, (s + 1) * size)
            offset, owner = table_ref[0:1, here], table_ref[1:2, here]
            own = jnp.where(owner == 0.0, rank_row(owner) - first, -1.0)
            ids = lax.broadcasted_iota(jnp.int32, (room, size), 0).astype(jnp.float32)
            picked = jnp.max(jnp.where(own == ids, offset, -1.0), axis=1, keepdims=True)
            pick[s * room : (s + 1) * room, :] = picked.astype(jnp.int32)

    ids = lax.broadcasted_iota(jnp.int32, (slots, reach), 1) + step * reach
    chosen = jnp.where(ids == pick[...], 1.0, 0.0).astype(jnp.bfloat16)
    res_high, res_low = split2(res_ref[...])
    pieces = (points_ref[:, :half], res_high, points_ref[:, half:], res_low)
    begin = 0
    for piece in pieces:
        columns = slice(begin, begin + piece.shape[1])
        begin += piece.shape[1]
        value = jnp.dot(chosen, piece, preferred_element_type=jnp.float32)
        total[:, columns] = jnp.where(step == 0, 0.0, total[:, columns]) + value

    @pl.when(step == pl.num_programs(0) - 1)
    def _():
        left_ref[...] = total[:, : half + outs].astype(jnp.bfloat16)
        right_ref[...] = total[:, half + outs :].astype(jnp.bfloat16)


def placed(table, sources, first, room):
    size = table.shape[1]
    rank = column_of(rank_row(table[1:2, :])) - first
    fits = (rank >= 0.0) & (rank < room)
    results = []
    for side, source in enumerate(sources):
        slot = jnp.where(fits, column_of(table[1 + side : 2 + side, :]) * room + rank, -1.0).astype(jnp.int32)
        lanes = lax.broadcasted_iota(jnp.int32, (size, source.shape[0]), 1)
        chosen = jnp.where(lanes == slot, 1.0, 0.0).astype(jnp.bfloat16)
        results.append(jnp.dot(chosen, source, preferred_element_type=jnp.float32))
    left, right = results
    half = left.shape[1]
    return left, right


def more_kernel(room, features, number_ref, table_ref, *refs):
    slots, (points_in, res_in, points_out, res_out) = refs[:4], refs[4:]
    half = features // 2
    sources = []
    for side in range(2):
        pair = [slots[2 * side + n][...] for n in range(2)]
        sources.append(jnp.concatenate([p.reshape(-1, p.shape[2]) for p in pair], axis=0))
    left, right = placed(table_ref[...], sources, (number_ref[0] * room).astype(jnp.float32), room)
    points_out[:, :half] = (left[:, :half] + points_in[:, :half].astype(jnp.float32)).astype(jnp.bfloat16)
    points_out[:, half:] = (right[:, :half] + points_in[:, half:].astype(jnp.float32)).astype(jnp.bfloat16)
    res_out[...] = res_in[...] + left[:, half:] + right[:, half:]


def gauss(inner, left, right, scale):
    return jnp.exp2((inner - left - right) * (2.0 * scale * 1.4426950408889634))


def main_kernel(steps, size, room, scale, list_ref, count_ref, offset_ref, round_ref, table_ref, *refs):
    slots, (base_points, base_res, points_hbm, res_hbm, coef_hbm, res_out, coef_out) = refs[:4], refs[4:11]
    chosen_ref, block_ref, tile_ref, norm_ref, work, inv_ref, cross_ref = refs[11:18]
    k_high, k_low, up_ref, both_ref, res, coef, in_sems, tile_sems, out_sems = refs[18:27]
    inner = refs[27:]
    features, outs = chosen_ref.shape[1], res.shape[1]
    half = features // 2
    count = steps * size
    devices = 2 * slots[0].shape[0]
    per_side = half + outs
    reach = tile_ref.shape[1]

    arriving = []
    for n in range(4):
        side, upper = n // 2, n % 2
        for j in range(devices // 2):
            begin = (upper * (devices // 2) + j) * steps * room
            place = k_low.at[pl.ds(begin, steps * room), pl.ds(side * per_side, per_side)]
            arriving.append(pltpu.make_async_copy(slots[n].at[j], place, in_sems.at[n * (devices // 2) + j]))

    def tile_copy(t, slot):
        return pltpu.make_async_copy(points_hbm.at[pl.ds(t * reach, reach)], tile_ref.at[slot], tile_sems.at[slot])

    tiles = k_high.shape[0] // reach
    for copy in arriving:
        copy.start()
    tile_copy(0, 0).start()
    whole_in = (
        pltpu.make_async_copy(res_hbm, res, out_sems.at[0]),
        pltpu.make_async_copy(coef_hbm, coef, out_sems.at[1]),
    )
    for copy in arriving:
        copy.wait()
    for copy in whole_in:
        copy.start()

    def block(s):
        return slice(s * size, (s + 1) * size)

    for s in range(steps):
        sources = []
        for side in range(2):
            columns = slice(side * per_side, (side + 1) * per_side)
            pieces = []
            for j in range(devices):
                begin = (j * steps + s) * room
                pieces.append(k_low[begin : begin + room, columns])
            sources.append(jnp.concatenate(pieces, axis=0))
        left, right = placed(table_ref[:, block(s)], sources, 0.0, room)
        chosen_ref[block(s), :half] = left[:, :half].astype(jnp.bfloat16)
        chosen_ref[block(s), half:] = right[:, :half].astype(jnp.bfloat16)
        up_ref[block(s), :] = left[:, half:] + right[:, half:]

    @pl.when(round_ref[0] > 1)
    def _():
        for s in range(steps):
            row_space = k_high.at[pl.ds(0, size), pl.ds(0, features)]
            res_space = inner[0].at[pl.ds(0, size), pl.ds(0, outs)]
            copies = (
                pltpu.make_async_copy(base_points.at[pl.ds(s * size, size)], row_space, in_sems.at[0]),
                pltpu.make_async_copy(base_res.at[pl.ds(s * size, size)], res_space, in_sems.at[1]),
            )
            for copy in copies:
                copy.start()
            for copy in copies:
                copy.wait()
            rows = chosen_ref[block(s), :].astype(jnp.float32) + k_high[:size, :features].astype(jnp.float32)
            chosen_ref[block(s), :] = rows.astype(jnp.bfloat16)
            up_ref[block(s), :] += inner[0][:size, :outs]

    eye = lax.broadcasted_iota(jnp.int32, (size, size), 0) == lax.broadcasted_iota(jnp.int32, (size, size), 1)
    columns = []
    for s in range(steps):
        product = lax.dot_general(chosen_ref[block(s), :], chosen_ref[block(s), :], NT, preferred_element_type=jnp.float32)
        diagonal = jnp.where(eye, product, 0.0)
        column = 0.5 * jnp.sum(diagonal, axis=1, keepdims=True)
        line = 0.5 * jnp.sum(diagonal, axis=0, keepdims=True)
        columns.append(column)
        norm_ref[:, block(s)] = line
        work[s] = gauss(product, column, line, scale) + jnp.where(eye, RIDGE, 0.0)
    pair = 0
    for s in range(steps):
        offset_column = column_of(table_ref[0:1, block(s)])
        for t in range(s):
            product = lax.dot_general(chosen_ref[block(s), :], chosen_ref[block(t), :], NT, preferred_element_type=jnp.float32)
            same = offset_column == table_ref[0:1, block(t)]
            cross_ref[pair] = gauss(product, columns[s], norm_ref[:, block(t)], scale) + jnp.where(same, RIDGE, 0.0)
            pair += 1

    def fill(t, carry):
        slot = lax.rem(t, 2)
        tile_copy(t, slot).wait()

        @pl.when(t + 1 < tiles)
        def _():
            tile_copy(t + 1, 1 - slot).start()

        lefts = []
        for begin in range(0, reach, PIECE):
            wide = tile_ref[slot, begin : begin + PIECE, :].astype(jnp.float32)
            lefts.append(0.5 * jnp.sum(wide * wide, axis=1, keepdims=True))

        def multiply(chunk, begin):
            piece = chosen_ref[chunk * CHUNK : (chunk + 1) * CHUNK, :]
            rows = tile_ref[slot, begin : begin + PIECE, :]
            value = lax.dot_general(rows, piece, NT, preferred_element_type=jnp.float32)
            inner[chunk % len(inner)][begin : begin + PIECE, :] = value

        for begin in range(0, reach, PIECE):
            multiply(0, begin)
        for chunk in range(count // CHUNK):
            columns = slice(chunk * CHUNK, (chunk + 1) * CHUNK)
            for number, begin in enumerate(range(0, reach, PIECE)):
                if chunk + 1 < count // CHUNK:
                    multiply(chunk + 1, begin)
                source = inner[chunk % len(inner)][begin : begin + PIECE, :]
                values = gauss(source, lefts[number], norm_ref[:, columns], scale) - 0.5
                rows = pl.ds(pl.multiple_of(t * reach + begin, PIECE), PIECE)
                high, low = split2(values)
                k_high[rows, columns] = high
                k_low[rows, columns] = low
        return carry

    lax.fori_loop(0, tiles, fill, 0)
    factor(steps, size, work, inv_ref)

    pair = 0
    total = None
    for s in range(steps):
        rhs = jnp.transpose(up_ref[block(s), :])
        for t in range(s):
            rhs = rhs - dot32(block_ref[:, block(t)], cross_ref[pair], NT)
            pair += 1
        update = dot32(dot32(rhs, inv_ref[s], NT), inv_ref[s])
        block_ref[:, block(s)] = update
        rows = jnp.transpose(update)
        up_ref[block(s), :] = rows
        high, low = split2(rows)
        both_ref[block(s), :outs] = high
        both_ref[block(s), outs : 2 * outs] = low
        part = jnp.sum(rows, axis=0, keepdims=True)
        total = part if total is None else total + part
    shift = 0.5 * total

    for copy in whole_in:
        copy.wait()
    for s in range(steps):

        def add_row(slot, carry):
            index = s * size + list_ref[s * size + slot]
            row = pl.ds(offset_ref[index], 1)
            update = up_ref[pl.ds(index, 1), :]
            coef[row, :] += update
            res[row, :] -= RIDGE * update
            return carry

        lax.fori_loop(0, count_ref[s], add_row, 0)
    coef_back = pltpu.make_async_copy(coef, coef_out, out_sems.at[1])
    coef_back.start()
    rows_each = 512

    def back(t):
        rows = pl.ds(pl.multiple_of(t * rows_each, rows_each), rows_each)
        return pltpu.make_async_copy(res.at[rows], res_out.at[rows], out_sems.at[0])

    def apply(t, carry):
        rows = pl.ds(pl.multiple_of(t * rows_each, rows_each), rows_each)
        upper = jnp.dot(k_high[rows, :], both_ref[:, : 2 * outs], preferred_element_type=jnp.float32)
        lower = jnp.dot(k_low[rows, :], both_ref[:, : 2 * outs], preferred_element_type=jnp.float32)
        value = (lower[:, outs:] + lower[:, :outs]) + upper[:, outs:] + upper[:, :outs]
        res[rows, :] = res[rows, :] - shift - value
        back(t).start()
        return carry

    lax.fori_loop(0, res.shape[0] // rows_each, apply, 0)
    coef_back.wait()
    pltpu.make_async_copy(res, res_out, out_sems.at[0]).wait()


def swap(block, bit, count):
    return lax.ppermute(block, "pts", [(i, i ^ bit) for i in range(count)])


def gather_slots(block, order, count):
    value = block[None]
    for bit in order[:-1]:
        value = jnp.concatenate([value, swap(value, bit, count)], axis=0)
    return [value, swap(value, order[-1], count)]


def route(order):
    names = [0]
    for bit in order:
        names = names + [name ^ bit for name in names]
    return names


def local(points, coefficients, residual, blocks):
    local_count, features = points.shape
    outs = residual.shape[1]
    steps, size = blocks.shape
    scale = 1.0 / features
    devices = lax.axis_size("pts")
    position = lax.axis_index("pts")
    count = steps * size
    pairs = steps * (steps - 1) // 2
    f32, bf16, i32 = jnp.float32, jnp.bfloat16, jnp.int32
    params = pltpu.CompilerParams(vmem_limit_bytes=63 * 2**20)
    reach = min(1024, local_count)

    def shape(dims, kind=f32):
        return jax.ShapeDtypeStruct(dims, kind)

    def whole(dims):
        return pl.BlockSpec(dims, lambda i, *_: (0,) * len(dims), pipeline_mode=pl.Buffered(1))

    mean = size // devices
    room = -(-(mean + 4 * int(mean**0.5 + 0.999)) // 16) * 16
    bits = [1 << b for b in range(devices.bit_length() - 1)]
    orders = (bits[1:] + bits[:1], bits[:0:-1] + bits[:1])
    owner = blocks // local_count
    offsets = blocks - position * local_count
    relative = (owner ^ position).reshape(-1)
    lines = [offsets.reshape(-1)]
    for order in orders:
        line = jnp.zeros_like(relative)
        for index, name in enumerate(route(order)):
            line = jnp.where(relative == name, index, line)
        lines.append(line)
    table = jnp.stack(lines + [jnp.zeros_like(relative)] * 5).astype(f32)

    smem = pl.BlockSpec(memory_space=pltpu.SMEM)
    vmem = pl.BlockSpec(memory_space=pltpu.VMEM)
    anywhere = pl.BlockSpec(memory_space=pl.ANY)
    side_shape = shape((steps * room, features // 2 + outs), bf16)

    def collect(number):
        sides = pl.pallas_call(
            functools.partial(select_kernel, steps, size, room),
            grid=(local_count // reach,),
            in_specs=[
                smem,
                whole((8, count)),
                pl.BlockSpec((reach, features), lambda i: (i, 0)),
                pl.BlockSpec((reach, outs), lambda i: (i, 0)),
            ],
            out_specs=[whole(side_shape.shape)] * 2,
            out_shape=[side_shape] * 2,
            scratch_shapes=[pltpu.VMEM((steps * room, 1), i32), pltpu.VMEM((steps * room, features + 2 * outs), f32)],
            compiler_params=params,
            name="select",
        )(number.reshape(1), table, points, residual)
        return [piece for side, order in zip(sides, orders) for piece in gather_slots(side, order, devices)]

    def more(number, state):
        half_devices = devices // 2
        return tuple(
            pl.pallas_call(
                functools.partial(more_kernel, room, features),
                grid=(steps,),
                in_specs=[smem, pl.BlockSpec((8, size), lambda s: (0, s))]
                + [pl.BlockSpec((half_devices, room, side_shape.shape[1]), lambda s: (0, s, 0))] * 4
                + [pl.BlockSpec((size, features), lambda s: (s, 0)), pl.BlockSpec((size, outs), lambda s: (s, 0))],
                out_specs=[pl.BlockSpec((size, features), lambda s: (s, 0)), pl.BlockSpec((size, outs), lambda s: (s, 0))],
                out_shape=[shape((count, features), bf16), shape((count, outs))],
                compiler_params=params,
                name="more",
            )(number.reshape(1), table, *collect(number), *state)
        )

    earlier = jnp.arange(size)[:, None] > jnp.arange(size)[None, :]
    rank = jnp.sum((owner[:, :, None] == owner[:, None, :]) & earlier, axis=2, dtype=i32)
    rounds = jnp.max(rank) // room + 1
    mine = owner == position
    amount = jnp.sum(mine, axis=1, dtype=i32)
    turn = jnp.where(mine, rank, -1)
    listed = jnp.sum(jnp.where(turn[:, None, :] == jnp.arange(size)[:, None], jnp.arange(size, dtype=i32), 0), axis=2, dtype=i32)

    slots = collect(jnp.zeros((), i32))
    empty = (jnp.zeros((count, features), bf16), jnp.zeros((count, outs), f32))
    base = lax.fori_loop(1, rounds, more, empty)

    residual_out, coefficients_out = pl.pallas_call(
        functools.partial(main_kernel, steps, size, room, scale),
        in_specs=[smem] * 4 + [vmem] + [anywhere] * 9,
        out_specs=[anywhere] * 2,
        out_shape=[shape((local_count, outs))] * 2,
        scratch_shapes=[
            pltpu.VMEM((count, features), bf16),
            pltpu.VMEM((outs, count), f32),
            pltpu.VMEM((2, reach, features), bf16),
            pltpu.VMEM((1, count), f32),
            pltpu.VMEM((steps, size, size), f32),
            pltpu.VMEM((steps, size, size), f32),
            pltpu.VMEM((pairs, size, size), f32),
            pltpu.VMEM((local_count, count), bf16),
            pltpu.VMEM((local_count, count), bf16),
            pltpu.VMEM((count, outs), f32),
            pltpu.VMEM((count, 2 * outs), bf16),
            pltpu.VMEM((local_count, outs), f32),
            pltpu.VMEM((local_count, outs), f32),
            pltpu.SemaphoreType.DMA((2 * devices,)),
            pltpu.SemaphoreType.DMA((2,)),
            pltpu.SemaphoreType.DMA((2,)),
        ]
        + [pltpu.VMEM((reach, CHUNK), f32)] * 3,
        compiler_params=params,
        name="main",
    )(
        listed.reshape(-1),
        amount,
        offsets.reshape(-1),
        rounds.reshape(1),
        table,
        *slots,
        *base,
        points,
        residual,
        coefficients,
    )
    return (coefficients_out, residual_out)


def solution(mesh):
    return jax.shard_map(
        local,
        mesh=mesh,
        in_specs=(P("pts", None), P("pts", "out"), P("pts", "out"), P()),
        out_specs=(P("pts", "out"), P("pts", "out")),
        check_vma=False,
    )
```

```python
import functools

import jax
import jax.numpy as jnp
from jax import lax
from jax.experimental import pallas as pl
from jax.experimental.pallas import tpu as pltpu
from jax.sharding import PartitionSpec as P

RIDGE = 0.5
PANEL = 128
GROUP = 8
SUB = 32
CHUNK = 256
PIECE = 1024
HIGHEST = lax.Precision.HIGHEST
NT = (((1,), (1,)), ((), ()))
TN = (((0,), (0,)), ((), ()))


def dot32(a, b, dims=(((1,), (0,)), ((), ()))):
    return lax.dot_general(a, b, dims, precision=HIGHEST, preferred_element_type=jnp.float32)


def spread_lane(tile, lane):
    return jnp.broadcast_to(tile[:, lane : lane + 1], tile.shape)


def spread_row(tile, row):
    return jnp.broadcast_to(tile[row : row + 1, :], tile.shape)


def eliminate(tiles, start, base):
    lanes = lax.broadcasted_iota(jnp.int32, (8, PANEL), 1)
    subs = lax.broadcasted_iota(jnp.int32, (8, PANEL), 0)
    first, offset = (start - base) // 8, start % 8
    in_group = (lanes >= start) & (lanes < start + GROUP)
    head = tiles[first]
    columns = [[spread_lane(tiles[t], start + q) for t in range(first, len(tiles))] for q in range(GROUP)]
    rows = []
    for q in range(GROUP):
        own = jnp.where(lanes == start + q, 1.0, 0.0)
        rows.append(jnp.where(in_group, own, spread_row(head, offset + q)))
    pivot = {}
    for m in range(GROUP):
        for q in range(m, GROUP):
            pivot[q, m] = spread_row(columns[m][0], offset + q)
    roots, scaled = [], []
    for m in range(GROUP):
        root = lax.rsqrt(pivot[m, m])
        inverse = root * root
        roots.append(root)
        factor = {q: pivot[q, m] * inverse for q in range(m + 1, GROUP)}
        for q in range(m + 1, GROUP):
            for n in range(m + 1, q + 1):
                pivot[q, n] = pivot[q, n] - factor[q] * pivot[n, m]
        for q in range(m + 1, GROUP):
            rows[q] = rows[q] - factor[q] * rows[m]
            columns[q] = [c - factor[q] * b for c, b in zip(columns[q], columns[m])]
        scaled.append(rows[m] * inverse)
    out = list(tiles)
    for t in range(first, len(tiles)):
        if t == first and offset + GROUP == 8:
            continue
        value = jnp.where(in_group, 0.0, tiles[t])
        for m in range(GROUP):
            value = value - columns[m][t - first] * scaled[m]
        out[t] = value
    top = jnp.where(subs < offset, head, out[first])
    for m in range(GROUP):
        top = jnp.where(subs == offset + m, rows[m] * roots[m], top)
    out[first] = top
    return out


def factor_panel(steps, strip_ref):
    for base in range(0, PANEL, SUB):
        strips = [[strip_ref[s, base + 8 * t : base + 8 * t + 8, :] for t in range(SUB // 8)] for s in range(steps)]
        for start in range(base, base + SUB, GROUP):
            strips = [eliminate(tiles, start, base) for tiles in strips]
        end = base + SUB
        for s in range(steps):
            strip = jnp.concatenate(strips[s], axis=0)
            lanes = lax.broadcasted_iota(jnp.int32, strip.shape, 1)
            subs = lax.broadcasted_iota(jnp.int32, strip.shape, 0)
            clear = jnp.where((lanes > subs + base) & (lanes < end), 0.0, strip)
            strip_ref[s, base:end, :] = jnp.where(lanes < end, clear, 0.0)
            if end < PANEL:
                lanes = lax.broadcasted_iota(jnp.int32, (PANEL - end, PANEL), 1)
                rest = jnp.where((lanes >= base) & (lanes < end), 0.0, strip_ref[s, end:, :])
                strip_ref[s, end:, :] = rest - dot32(strip[:, end:], clear, TN)


def factor(steps, size, work, inv_ref, strip_ref):
    panels = size // PANEL

    def panel(k, carry):
        here = pl.ds(pl.multiple_of(k * PANEL, PANEL), PANEL)
        for s in range(steps):
            strip_ref[s] = work[s, here, here]
        factor_panel(steps, strip_ref)
        for s in range(steps):
            inv_ref[s, here, here] = strip_ref[s]
        for fixed in range(panels):

            @pl.when(k == fixed)
            def _():
                low, high = fixed * PANEL, (fixed + 1) * PANEL
                for s in range(steps):
                    tri = strip_ref[s]
                    if high < size:
                        inv_ref[s, low:high, high:] = jnp.zeros((PANEL, size - high), jnp.float32)
                        below = dot32(work[s, high:, low:high], tri, NT)
                        work[s, high:, low:high] = below
                        work[s, high:, high:] = work[s, high:, high:] - dot32(below, below, NT)
                    if low > 0:
                        left = dot32(work[s, low:high, :low], inv_ref[s, :low, :low])
                        inv_ref[s, low:high, :low] = -dot32(tri, left)

        return carry

    lax.fori_loop(0, panels, panel, 0)


def column_of(row):
    size = row.shape[1]
    eye = lax.broadcasted_iota(jnp.int32, (size, size), 0) == lax.broadcasted_iota(jnp.int32, (size, size), 1)
    return jnp.sum(jnp.where(eye, row, 0.0), axis=1, keepdims=True)


def rank_row(owner):
    size = owner.shape[1]
    earlier = lax.broadcasted_iota(jnp.int32, (size, size), 0) < lax.broadcasted_iota(jnp.int32, (size, size), 1)
    return jnp.sum(jnp.where((column_of(owner) == owner) & earlier, 1.0, 0.0), axis=0, keepdims=True)


def split2(value):
    high = value.astype(jnp.bfloat16)
    return high, (value - high.astype(jnp.float32)).astype(jnp.bfloat16)


def select_kernel(steps, size, room, number_ref, table_ref, points_ref, res_ref, own_ref, pick, total):
    step = pl.program_id(0)
    reach = points_ref.shape[0]
    slots = steps * room

    @pl.when(step == 0)
    def _():
        first = (number_ref[0] * room).astype(jnp.float32)
        for s in range(steps):
            here = slice(s * size, (s + 1) * size)
            offset, owner = table_ref[0:1, here], table_ref[1:2, here]
            own = jnp.where(owner == 0.0, rank_row(owner) - first, -1.0)
            ids = lax.broadcasted_iota(jnp.int32, (room, size), 0).astype(jnp.float32)
            picked = jnp.max(jnp.where(own == ids, offset, -1.0), axis=1, keepdims=True)
            pick[s * room : (s + 1) * room, :] = picked.astype(jnp.int32)

    ids = lax.broadcasted_iota(jnp.int32, (slots, reach), 1) + step * reach
    chosen = jnp.where(ids == pick[...], 1.0, 0.0).astype(jnp.bfloat16)
    res_high, res_low = split2(res_ref[...])
    pieces = (points_ref[...], res_high, res_low)
    begin = 0
    for piece in pieces:
        columns = slice(begin, begin + piece.shape[1])
        begin += piece.shape[1]
        value = jnp.dot(chosen, piece, preferred_element_type=jnp.float32)
        total[:, columns] = jnp.where(step == 0, 0.0, total[:, columns]) + value

    @pl.when(step == pl.num_programs(0) - 1)
    def _():
        own_ref[...] = total[...].astype(jnp.bfloat16)


def placed(table, source, first, room):
    size = table.shape[1]
    rank = column_of(rank_row(table[1:2, :])) - first
    fits = (rank >= 0.0) & (rank < room)
    slot = jnp.where(fits, column_of(table[1:2, :]) * room + rank, -1.0).astype(jnp.int32)
    lanes = lax.broadcasted_iota(jnp.int32, (size, source.shape[0]), 1)
    chosen = jnp.where(lanes == slot, 1.0, 0.0).astype(jnp.bfloat16)
    return jnp.dot(chosen, source, preferred_element_type=jnp.float32)


def more_kernel(room, features, number_ref, table_ref, slots, points_in, res_in, points_out, res_out):
    source = slots[...].reshape(-1, slots.shape[2])
    value = placed(table_ref[...], source, (number_ref[0] * room).astype(jnp.float32), room)
    outs = res_in.shape[1]
    points_out[...] = (value[:, :features] + points_in[...].astype(jnp.float32)).astype(jnp.bfloat16)
    res_out[...] = res_in[...] + value[:, features : features + outs] + value[:, features + outs :]


def gauss(inner, left, right, scale):
    return jnp.exp2((inner - left - right) * (2.0 * scale * 1.4426950408889634))


def main_kernel(steps, size, room, scale, devices, plan, list_ref, count_ref, offset_ref, round_ref, table_ref, *refs):
    slots, refs = refs[: len(plan)], refs[len(plan) :]
    base_points, base_res, points_hbm, res_hbm, coef_hbm, res_out, coef_out = refs[:7]
    chosen_ref, block_ref, tile_ref, norm_ref, work, inv_ref, cross_ref = refs[7:14]
    k_high, k_low, up_ref, both_ref, res, coef, in_sems, tile_sems, out_sems = refs[14:23]
    strip_ref, inner = refs[23], refs[24:]
    features, outs = chosen_ref.shape[1], res.shape[1]
    count = steps * size
    reach = tile_ref.shape[1]
    width = features + 2 * outs

    arriving = []
    for n, (name, begin) in enumerate(plan):
        place = k_low.at[pl.ds(name * steps * room, steps * room), pl.ds(begin, slots[n].shape[1])]
        arriving.append(pltpu.make_async_copy(slots[n], place, in_sems.at[n]))

    def tile_copy(t, slot):
        return pltpu.make_async_copy(points_hbm.at[pl.ds(t * reach, reach)], tile_ref.at[slot], tile_sems.at[slot])

    tiles = k_high.shape[0] // reach
    for copy in arriving:
        copy.start()
    tile_copy(0, 0).start()
    whole_in = (
        pltpu.make_async_copy(res_hbm, res, out_sems.at[0]),
        pltpu.make_async_copy(coef_hbm, coef, out_sems.at[1]),
    )
    for copy in arriving:
        copy.wait()
    for copy in whole_in:
        copy.start()

    def block(s):
        return slice(s * size, (s + 1) * size)

    for s in range(steps):
        pieces = []
        for j in range(devices):
            begin = (j * steps + s) * room
            pieces.append(k_low[begin : begin + room, :width])
        value = placed(table_ref[:, block(s)], jnp.concatenate(pieces, axis=0), 0.0, room)
        chosen_ref[block(s), :] = value[:, :features].astype(jnp.bfloat16)
        up_ref[block(s), :] = value[:, features : features + outs] + value[:, features + outs :]

    @pl.when(round_ref[0] > 1)
    def _():
        for s in range(steps):
            row_space = k_high.at[pl.ds(0, size), pl.ds(0, features)]
            res_space = inner[0].at[pl.ds(0, size), pl.ds(0, outs)]
            copies = (
                pltpu.make_async_copy(base_points.at[pl.ds(s * size, size)], row_space, in_sems.at[0]),
                pltpu.make_async_copy(base_res.at[pl.ds(s * size, size)], res_space, in_sems.at[1]),
            )
            for copy in copies:
                copy.start()
            for copy in copies:
                copy.wait()
            rows = chosen_ref[block(s), :].astype(jnp.float32) + k_high[:size, :features].astype(jnp.float32)
            chosen_ref[block(s), :] = rows.astype(jnp.bfloat16)
            up_ref[block(s), :] += inner[0][:size, :outs]

    eye = lax.broadcasted_iota(jnp.int32, (size, size), 0) == lax.broadcasted_iota(jnp.int32, (size, size), 1)
    columns = []
    for s in range(steps):
        product = lax.dot_general(chosen_ref[block(s), :], chosen_ref[block(s), :], NT, preferred_element_type=jnp.float32)
        diagonal = jnp.where(eye, product, 0.0)
        column = 0.5 * jnp.sum(diagonal, axis=1, keepdims=True)
        line = 0.5 * jnp.sum(diagonal, axis=0, keepdims=True)
        columns.append(column)
        norm_ref[:, block(s)] = line
        work[s] = gauss(product, column, line, scale) + jnp.where(eye, RIDGE, 0.0)
    pair = 0
    for s in range(steps):
        offset_column = column_of(table_ref[0:1, block(s)])
        for t in range(s):
            product = lax.dot_general(chosen_ref[block(s), :], chosen_ref[block(t), :], NT, preferred_element_type=jnp.float32)
            same = offset_column == table_ref[0:1, block(t)]
            cross_ref[pair] = gauss(product, columns[s], norm_ref[:, block(t)], scale) + jnp.where(same, RIDGE, 0.0)
            pair += 1

    def fill(t, carry):
        slot = lax.rem(t, 2)
        tile_copy(t, slot).wait()

        @pl.when(t + 1 < tiles)
        def _():
            tile_copy(t + 1, 1 - slot).start()

        lefts = []
        for begin in range(0, reach, PIECE):
            wide = tile_ref[slot, begin : begin + PIECE, :].astype(jnp.float32)
            lefts.append(0.5 * jnp.sum(wide * wide, axis=1, keepdims=True))

        def multiply(chunk, begin):
            piece = chosen_ref[chunk * CHUNK : (chunk + 1) * CHUNK, :]
            rows = tile_ref[slot, begin : begin + PIECE, :]
            value = lax.dot_general(rows, piece, NT, preferred_element_type=jnp.float32)
            inner[chunk % len(inner)][begin : begin + PIECE, :] = value

        for begin in range(0, reach, PIECE):
            multiply(0, begin)
        for chunk in range(count // CHUNK):
            columns = slice(chunk * CHUNK, (chunk + 1) * CHUNK)
            for number, begin in enumerate(range(0, reach, PIECE)):
                if chunk + 1 < count // CHUNK:
                    multiply(chunk + 1, begin)
                source = inner[chunk % len(inner)][begin : begin + PIECE, :]
                values = gauss(source, lefts[number], norm_ref[:, columns], scale) - 0.5
                rows = pl.ds(pl.multiple_of(t * reach + begin, PIECE), PIECE)
                high, low = split2(values)
                k_high[rows, columns] = high
                k_low[rows, columns] = low
        return carry

    lax.fori_loop(0, tiles, fill, 0)
    factor(steps, size, work, inv_ref, strip_ref)

    pair = 0
    total = None
    for s in range(steps):
        rhs = jnp.transpose(up_ref[block(s), :])
        for t in range(s):
            rhs = rhs - dot32(block_ref[:, block(t)], cross_ref[pair], NT)
            pair += 1
        update = dot32(dot32(rhs, inv_ref[s], NT), inv_ref[s])
        block_ref[:, block(s)] = update
        rows = jnp.transpose(update)
        up_ref[block(s), :] = rows
        high, low = split2(rows)
        both_ref[block(s), :outs] = high
        both_ref[block(s), outs : 2 * outs] = low
        part = jnp.sum(rows, axis=0, keepdims=True)
        total = part if total is None else total + part
    shift = 0.5 * total

    for copy in whole_in:
        copy.wait()
    for s in range(steps):

        def add_row(slot, carry):
            index = s * size + list_ref[s * size + slot]
            row = pl.ds(offset_ref[index], 1)
            update = up_ref[pl.ds(index, 1), :]
            coef[row, :] += update
            res[row, :] -= RIDGE * update
            return carry

        lax.fori_loop(0, count_ref[s], add_row, 0)
    coef_back = pltpu.make_async_copy(coef, coef_out, out_sems.at[1])
    coef_back.start()
    rows_each = 512

    def back(t):
        rows = pl.ds(pl.multiple_of(t * rows_each, rows_each), rows_each)
        return pltpu.make_async_copy(res.at[rows], res_out.at[rows], out_sems.at[0])

    def apply(t, carry):
        rows = pl.ds(pl.multiple_of(t * rows_each, rows_each), rows_each)
        upper = jnp.dot(k_high[rows, :], both_ref[:, : 2 * outs], preferred_element_type=jnp.float32)
        lower = jnp.dot(k_low[rows, :], both_ref[:, : 2 * outs], preferred_element_type=jnp.float32)
        value = (lower[:, outs:] + lower[:, :outs]) + upper[:, outs:] + upper[:, :outs]
        res[rows, :] = res[rows, :] - shift - value
        back(t).start()
        return carry

    lax.fori_loop(0, res.shape[0] // rows_each, apply, 0)
    coef_back.wait()
    pltpu.make_async_copy(res, res_out, out_sems.at[0]).wait()


def swap(block, bit, count):
    return lax.ppermute(block, "pts", [(i, i ^ bit) for i in range(count)])


def gather_slots(own, count):
    bits = [1 << b for b in range(count.bit_length() - 1)]
    pieces = [(own, 0, 0)]
    outer = bits[1:]
    if len(outer) == 2:
        half = own.shape[1] // 2
        sides = [swap(own, bit, count) for bit in outer]
        corner = outer[0] ^ outer[1]
        pieces += [(side, bit, 0) for side, bit in zip(sides, outer)]
        pieces.append((swap(sides[0][:, :half], outer[1], count), corner, 0))
        pieces.append((swap(sides[1][:, half:], outer[0], count), corner, half))
        outer = []
    for bit in outer + bits[:1]:
        pieces += [(swap(piece, bit, count), name ^ bit, begin) for piece, name, begin in pieces]
    return pieces


def local(points, coefficients, residual, blocks):
    local_count, features = points.shape
    outs = residual.shape[1]
    steps, size = blocks.shape
    scale = 1.0 / features
    devices = lax.axis_size("pts")
    position = lax.axis_index("pts")
    count = steps * size
    pairs = steps * (steps - 1) // 2
    f32, bf16, i32 = jnp.float32, jnp.bfloat16, jnp.int32
    params = pltpu.CompilerParams(vmem_limit_bytes=63 * 2**20)
    reach = min(1024, local_count)

    def shape(dims, kind=f32):
        return jax.ShapeDtypeStruct(dims, kind)

    def whole(dims):
        return pl.BlockSpec(dims, lambda i, *_: (0,) * len(dims), pipeline_mode=pl.Buffered(1))

    mean = size // devices
    room = -(-(mean + 4 * int(mean**0.5 + 0.999)) // 16) * 16
    owner = blocks // local_count
    offsets = blocks - position * local_count
    relative = (owner ^ position).reshape(-1)
    table = jnp.stack([offsets.reshape(-1), relative] + [jnp.zeros_like(relative)] * 6).astype(f32)

    smem = pl.BlockSpec(memory_space=pltpu.SMEM)
    vmem = pl.BlockSpec(memory_space=pltpu.VMEM)
    anywhere = pl.BlockSpec(memory_space=pl.ANY)
    width = features + 2 * outs
    own_shape = shape((steps * room, width), bf16)

    def collect(number):
        own = pl.pallas_call(
            functools.partial(select_kernel, steps, size, room),
            grid=(local_count // reach,),
            in_specs=[
                smem,
                whole((8, count)),
                pl.BlockSpec((reach, features), lambda i: (i, 0)),
                pl.BlockSpec((reach, outs), lambda i: (i, 0)),
            ],
            out_specs=whole(own_shape.shape),
            out_shape=own_shape,
            scratch_shapes=[pltpu.VMEM((steps * room, 1), i32), pltpu.VMEM((steps * room, width), f32)],
            compiler_params=params,
            name="select",
        )(number.reshape(1), table, points, residual)
        return gather_slots(own, devices)

    def more(number, state):
        everyone = jnp.zeros((devices, steps * room, width), bf16)
        for piece, name, begin in collect(number):
            everyone = everyone.at[name, :, begin : begin + piece.shape[1]].set(piece)
        return tuple(
            pl.pallas_call(
                functools.partial(more_kernel, room, features),
                grid=(steps,),
                in_specs=[
                    smem,
                    pl.BlockSpec((8, size), lambda s: (0, s)),
                    pl.BlockSpec((devices, room, width), lambda s: (0, s, 0)),
                    pl.BlockSpec((size, features), lambda s: (s, 0)),
                    pl.BlockSpec((size, outs), lambda s: (s, 0)),
                ],
                out_specs=[pl.BlockSpec((size, features), lambda s: (s, 0)), pl.BlockSpec((size, outs), lambda s: (s, 0))],
                out_shape=[shape((count, features), bf16), shape((count, outs))],
                compiler_params=params,
                name="more",
            )(number.reshape(1), table, everyone, *state)
        )

    earlier = jnp.arange(size)[:, None] > jnp.arange(size)[None, :]
    rank = jnp.sum((owner[:, :, None] == owner[:, None, :]) & earlier, axis=2, dtype=i32)
    rounds = jnp.max(rank) // room + 1
    mine = owner == position
    amount = jnp.sum(mine, axis=1, dtype=i32)
    turn = jnp.where(mine, rank, -1)
    listed = jnp.sum(jnp.where(turn[:, None, :] == jnp.arange(size)[:, None], jnp.arange(size, dtype=i32), 0), axis=2, dtype=i32)

    slots = collect(jnp.zeros((), i32))
    plan = tuple(piece[1:] for piece in slots)
    empty = (jnp.zeros((count, features), bf16), jnp.zeros((count, outs), f32))
    base = lax.fori_loop(1, rounds, more, empty)

    residual_out, coefficients_out = pl.pallas_call(
        functools.partial(main_kernel, steps, size, room, scale, devices, plan),
        in_specs=[smem] * 4 + [vmem] + [anywhere] * (len(plan) + 5),
        out_specs=[anywhere] * 2,
        out_shape=[shape((local_count, outs))] * 2,
        scratch_shapes=[
            pltpu.VMEM((count, features), bf16),
            pltpu.VMEM((outs, count), f32),
            pltpu.VMEM((2, reach, features), bf16),
            pltpu.VMEM((1, count), f32),
            pltpu.VMEM((steps, size, size), f32),
            pltpu.VMEM((steps, size, size), f32),
            pltpu.VMEM((pairs, size, size), f32),
            pltpu.VMEM((local_count, count), bf16),
            pltpu.VMEM((local_count, count), bf16),
            pltpu.VMEM((count, outs), f32),
            pltpu.VMEM((count, 2 * outs), bf16),
            pltpu.VMEM((local_count, outs), f32),
            pltpu.VMEM((local_count, outs), f32),
            pltpu.SemaphoreType.DMA((len(plan),)),
            pltpu.SemaphoreType.DMA((2,)),
            pltpu.SemaphoreType.DMA((2,)),
        ]
        + [pltpu.VMEM((steps, PANEL, PANEL), f32)]
        + [pltpu.VMEM((reach, CHUNK), f32)] * 3,
        compiler_params=params,
        name="main",
    )(
        listed.reshape(-1),
        amount,
        offsets.reshape(-1),
        rounds.reshape(1),
        table,
        *(piece[0] for piece in slots),
        *base,
        points,
        residual,
        coefficients,
    )
    return (coefficients_out, residual_out)


def solution(mesh):
    return jax.shard_map(
        local,
        mesh=mesh,
        in_specs=(P("pts", None), P("pts", "out"), P("pts", "out"), P()),
        out_specs=(P("pts", "out"), P("pts", "out")),
        check_vma=False,
    )
```
